32 devices in a mesh: dom: 8 (over z, y), sub: 4 (over x, core).
Axes of the slice: x: 2, y: 2, z: 4, core: 2. Of those that a mesh axis runs over, the one named last changes fastest.
Arguments:
- node_state: bfloat16 [64, 32768], P(None, ('dom', 'sub')), may hold values from -6 to 6
- edge_state: bfloat16 [64, 98304], P(None, ('dom', 'sub')), may hold values from -6 to 6
- senders: int32 [98304], P(('dom', 'sub')), may hold values from 0 to 2559, as said below
- receivers: int32 [98304], P(('dom', 'sub')), may hold values from 0 to 1023
- send_index: int32 [32, 12, 128], P(('dom', 'sub')), may hold values from -1 to 1023, as said below
- node_cotangent: bfloat16 [64, 32768], P(None, ('dom', 'sub')), may hold values from -6 to 6
- edge_cotangent: bfloat16 [64, 98304], P(None, ('dom', 'sub')), may hold values from -6 to 6
- edge_first: bfloat16 [192, 64], replicated, may hold values from -0.4375 to 0.4375
- edge_bias: float32 [64], replicated, may hold values from -3 to 3
- edge_second: bfloat16 [64, 64], replicated, may hold values from -0.75 to 0.75
- edge_gain: float32 [64], replicated, may hold values from 0.1 to 1.9
- edge_shift: float32 [64], replicated, may hold values from -3 to 3
- node_first: bfloat16 [128, 64], replicated, may hold values from -0.5 to 0.5
- node_bias: float32 [64], replicated, may hold values from -3 to 3
- node_second: bfloat16 [64, 64], replicated, may hold values from -0.75 to 0.75
- node_gain: float32 [64], replicated, may hold values from 0.1 to 1.9
Outputs:
- delta_state: bfloat16 [64, 32768], P(None, ('dom', 'sub'))
- delta_edges: bfloat16 [64, 98304], P(None, ('dom', 'sub'))
- delta_edgefirst: float32 [192, 64], replicated
- delta_edgebias: float32 [64], replicated
- delta_edgesecond: float32 [64, 64], replicated
- delta_edgegain: float32 [64], replicated
- delta_edgeshift: float32 [64], replicated
- delta_nodefirst: float32 [128, 64], replicated
- delta_nodebias: float32 [64], replicated
- delta_nodesecond: float32 [64, 64], replicated
- delta_nodegain: float32 [64], replicated
- delta_nodeshift: float32 [64], replicated
The draws below stay inside these ranges and needn't reach their ends.
Inputs may be any that keep to these rules, and one draw needn't show every extreme that they name: `send_index`: block k = o * 4 + t of partition p = d * 4 + s lists own cells that p sends to the partition at dom index d + o - 1 and sub index t: live entries first, then -1. Blocks towards a dom index outside the mesh, and block 4 + s, hold only -1; every other block holds 32 to 128 live entries. Some partition receives a full block from every partition that sends to it. `senders`: an entry below 1024 is an own cell. An entry 1024 + k * 128 + j with k = o * 4 + u names ghost slot j of block k: the j-th entry of block o * 4 + s of the partition at dom index d + 1 - o and sub index u, and that entry is live.
All inputs are finite; a program needn't handle non-finite values.
Results may differ from the reference program's by a relative error of at most 0.0095.
Values may be sent and summed in bfloat16 or wider, within the bound.
No kernel may reach another device: no remote copies, remote signals or barrier semaphores. Data moves between devices by JAX's collectives and lax.ppermute only.
A program may use at most 64 MiB of HBM per device.

```python
import math
import jax
import jax.numpy as jnp
from jax import lax

D = 64
HIDDEN_SIZE = 64
CELLS_DEV = 1024
HALO = 128
FACES_DEV = 3072
PARTITIONS = 32
PEERS = 12
GHOST = 1536
CELLS = 32768
FACES = 98304
N_DOM = 8
N_SUB = 4


def halo_counts(key):
    base_key = jax.random.fold_in(key, 7)
    count_key, target_key = jax.random.split(base_key)
    live_count = jax.random.randint(count_key, (PARTITIONS, PEERS), HALO // 4, HALO + 1)
    partition = jnp.arange(PARTITIONS, dtype=jnp.int32)[:, None]
    peer_slot = jnp.arange(PEERS, dtype=jnp.int32)[None, :]
    target_row = partition // N_SUB + peer_slot // N_SUB - 1
    sub_here = partition % N_SUB
    exists = (target_row >= 0) & (target_row < N_DOM) & jnp.logical_not((peer_slot // N_SUB == 1) & (peer_slot % N_SUB == sub_here))
    chosen = jax.random.randint(target_key, (), N_SUB, PARTITIONS)
    target = target_row * N_SUB + peer_slot % N_SUB
    receives_full = target == chosen
    counts = jnp.where(receives_full, HALO, live_count)
    return jnp.where(exists, counts, 0).astype(jnp.int32)


def draw_send_index(key, part):
    counts = halo_counts(key)
    cell_draw = jax.random.randint(jax.random.fold_in(key, 11), (PARTITIONS, PEERS, HALO), 0, CELLS_DEV)
    slot_position = jnp.arange(HALO, dtype=jnp.int32)[None, None, :]
    return jnp.where(slot_position < counts[:, :, None], cell_draw, -1).astype(jnp.int32)


def draw_senders(key, part):
    counts = halo_counts(key)
    partition = jnp.arange(PARTITIONS, dtype=jnp.int32)[:, None]
    peer_slot = jnp.arange(PEERS, dtype=jnp.int32)[None, :]
    source_row = partition // N_SUB + 1 - peer_slot // N_SUB
    source_ok = (source_row >= 0) & (source_row < N_DOM)
    source = jnp.clip(source_row * N_SUB + peer_slot % N_SUB, 0, PARTITIONS - 1)
    mirror_slot = peer_slot // N_SUB * N_SUB + partition % N_SUB
    incoming = jnp.where(source_ok, counts[source, mirror_slot], 0)
    key_list = jax.random.split(jax.random.fold_in(key, 23), 4)
    local_cells = jax.random.randint(key_list[0], (PARTITIONS, FACES_DEV), 0, CELLS_DEV)
    chosen_peer = jax.random.randint(key_list[1], (PARTITIONS, FACES_DEV), 0, PEERS)
    position = jax.random.randint(key_list[2], (PARTITIONS, FACES_DEV), 0, HALO)
    want_ghost = jax.random.randint(key_list[3], (PARTITIONS, FACES_DEV), 0, 8) == 0
    face_number = jnp.arange(FACES_DEV, dtype=jnp.int32)[None, :]
    last_face = face_number == FACES_DEV - 1
    chosen_peer = jnp.where(last_face, PEERS - 1, chosen_peer)
    available = jnp.take_along_axis(incoming, chosen_peer, axis=1)
    position = jnp.where(last_face, available - 1, position % jnp.maximum(available, 1))
    use_ghost = (want_ghost | last_face) & (available > 0)
    ghost_index = CELLS_DEV + chosen_peer * HALO + position
    return jnp.where(use_ghost, ghost_index, local_cells).reshape(-1).astype(jnp.int32)


def place_ends(values, own_key, low, largest):
    shape = values.shape
    spot = [jax.random.randint(jax.random.fold_in(own_key, axis), (), 0, shape[axis]) for axis in range(len(shape))]
    values = values.at[tuple(spot)].set(low)
    longest = shape.index(max(shape))
    spot[longest] = (spot[longest] + 1) % shape[longest]
    return values.at[tuple(spot)].set(largest)


def level_of(key, extent, cuts, low, largest):
    level, own = 1.0, jax.random.fold_in(key, 6)
    for axis_at, shards_of in cuts:
        heights = jnp.exp(jax.random.uniform(jax.random.fold_in(own, axis_at), (shards_of,), jnp.float32, low / len(cuts), largest / len(cuts)))
        level = level * jnp.repeat(heights, extent[axis_at] // shards_of).reshape([-1 if axis == axis_at else 1 for axis in range(len(extent))])
    return level


def scatter_about(rng, shape, deviation, most, cuts=(), kind=jnp.bfloat16):
    factor_of = level_of(rng, shape, cuts, -0.22, 0.18) if cuts else 1.0
    values = jax.random.normal(rng, shape, jnp.float32) * deviation * factor_of
    return jnp.minimum(jnp.maximum(values, -most), most).astype(kind)


def setup_inputs(seed: int = 0) -> dict:
    splits = jax.random.split(jax.random.key(seed), 17)
    return {
        "node_state": scatter_about(splits[0], (D, CELLS), 1.0, 6.0, ((1, 32),)),
        "edge_state": scatter_about(splits[1], (D, FACES), 1.0, 6.0, ((1, 32),)),
        "senders": draw_senders(jax.random.fold_in(splits[16], 71), 0),
        "receivers": place_ends(jax.random.randint(splits[3], (FACES,), 0, CELLS_DEV), jax.random.fold_in(splits[3], 1), 0, CELLS_DEV - 1).astype(jnp.int32),
        "send_index": draw_send_index(jax.random.fold_in(splits[16], 71), 0),
        "node_cotangent": scatter_about(splits[5], (D, CELLS), 1.0, 6.0, ((1, 32),)),
        "edge_cotangent": scatter_about(splits[6], (D, FACES), 1.0, 6.0, ((1, 32),)),
        "edge_first": scatter_about(splits[7], (3 * D, HIDDEN_SIZE), (3 * D) ** -0.5, 0.4375),
        "edge_bias": scatter_about(splits[8], (HIDDEN_SIZE,), 0.5, 3.0, (), jnp.float32),
        "edge_second": scatter_about(splits[9], (HIDDEN_SIZE, D), HIDDEN_SIZE ** -0.5, 0.75),
        "edge_gain": jnp.clip(1.0 + 0.18 * jax.random.normal(splits[10], (D,), jnp.float32), 0.1, 1.9),
        "edge_shift": scatter_about(splits[11], (D,), 0.5, 3.0, (), jnp.float32),
        "node_first": scatter_about(splits[12], (2 * D, HIDDEN_SIZE), (2 * D) ** -0.5, 0.5),
        "node_bias": scatter_about(splits[13], (HIDDEN_SIZE,), 0.5, 3.0, (), jnp.float32),
        "node_second": scatter_about(splits[14], (HIDDEN_SIZE, D), HIDDEN_SIZE ** -0.5, 0.75),
        "node_gain": jnp.clip(1.0 + 0.18 * jax.random.normal(splits[15], (D,), jnp.float32), 0.1, 1.9),
    }


EPSILON = 1e-05

def contract_first(first_operand, second_operand):
    return lax.dot_general(first_operand, second_operand, (((0,), (0,)), ((), ())), preferred_element_type=jnp.float32)

def contract_last(first_operand, second_operand):
    return lax.dot_general(first_operand, second_operand, (((1,), (1,)), ((), ())), preferred_element_type=jnp.float32)

def sigmoid_linear(values):
    return values * jax.nn.sigmoid(values)

def sigmoid_slope(values):
    logistic = jax.nn.sigmoid(values)
    return logistic * (1.0 + values * (1.0 - logistic))

def standardize(values):
    centered = values - lax.optimization_barrier(jnp.mean(values, axis=0, keepdims=True))
    spread = lax.rsqrt(lax.optimization_barrier(jnp.mean(centered * centered, axis=0, keepdims=True)) + EPSILON)
    return (centered * spread, spread)

def normalize_back(upstream, scaled, spread, gain_vector):
    gain_delta = lax.optimization_barrier(jnp.sum(upstream * scaled, axis=1))
    shift_delta = lax.optimization_barrier(jnp.sum(upstream, axis=1))
    weighted = upstream * gain_vector[:, None]
    result = spread * (weighted - lax.optimization_barrier(jnp.mean(weighted, axis=0, keepdims=True)) - scaled * lax.optimization_barrier(jnp.mean(weighted * scaled, axis=0, keepdims=True)))
    return (result, gain_delta, shift_delta)

def local_backward(extended, node_state, edge_state, senders, receivers, node_cotangent, edge_cotangent, edge_first, edge_bias, edge_second, edge_gain, edge_shift, node_first, node_bias, node_second, node_gain):
    features, cell_count = node_state.shape
    sender_rows = jnp.take(extended, senders, axis=1)
    receiver_rows = jnp.take(node_state, receivers, axis=1)
    stacked = jnp.concatenate([sender_rows, receiver_rows, edge_state], axis=0)
    edge_linear = contract_first(edge_first, stacked) + edge_bias[:, None]
    edge_active = sigmoid_linear(edge_linear).astype(jnp.bfloat16)
    edge_output = contract_first(edge_second, edge_active)
    edge_scaled, edge_spread = standardize(edge_output)
    message = (edge_scaled * edge_gain[:, None] + edge_shift[:, None]).astype(jnp.bfloat16)
    summed = jnp.zeros((features, cell_count), jnp.float32).at[:, receivers].add(message.astype(jnp.float32))
    node_input = jnp.concatenate([node_state, summed.astype(jnp.bfloat16)], axis=0)
    node_linear = contract_first(node_first, node_input) + node_bias[:, None]
    node_active = sigmoid_linear(node_linear).astype(jnp.bfloat16)
    node_output = contract_first(node_second, node_active)
    node_scaled, node_spread = standardize(node_output)
    upstream = node_cotangent.astype(jnp.float32)
    node_delta, nodegain_delta, nodeshift_delta = normalize_back(upstream, node_scaled, node_spread, node_gain)
    node_delta = node_delta.astype(jnp.bfloat16)
    nodesecond_delta = contract_last(node_active, node_delta)
    node_hidden = jnp.dot(node_second, node_delta, preferred_element_type=jnp.float32) * sigmoid_slope(node_linear)
    nodebias_delta = lax.optimization_barrier(jnp.sum(node_hidden, axis=1))
    node_hidden = node_hidden.astype(jnp.bfloat16)
    nodefirst_delta = contract_last(node_input, node_hidden)
    node_back = jnp.dot(node_first, node_hidden, preferred_element_type=jnp.float32)
    message_delta = edge_cotangent.astype(jnp.float32) + jnp.take(node_back[features:], receivers, axis=1)
    edge_delta, edgegain_delta, edgeshift_delta = normalize_back(message_delta, edge_scaled, edge_spread, edge_gain)
    edge_delta = edge_delta.astype(jnp.bfloat16)
    edgesecond_delta = contract_last(edge_active, edge_delta)
    edge_hidden = jnp.dot(edge_second, edge_delta, preferred_element_type=jnp.float32) * sigmoid_slope(edge_linear)
    edgebias_delta = lax.optimization_barrier(jnp.sum(edge_hidden, axis=1))
    edge_hidden = edge_hidden.astype(jnp.bfloat16)
    edgefirst_delta = contract_last(stacked, edge_hidden)
    edge_back = jnp.dot(edge_first, edge_hidden, preferred_element_type=jnp.float32)
    edge_result = (edge_cotangent.astype(jnp.float32) + edge_back[2 * features:]).astype(jnp.bfloat16)
    scattered = jnp.zeros(extended.shape, jnp.float32).at[:, senders].add(edge_back[:features])
    local_delta = scattered[:, :cell_count].at[:, receivers].add(edge_back[features:2 * features]) + node_back[:features] + upstream
    ghost_delta = scattered[:, cell_count:]
    partials = (edgefirst_delta, edgebias_delta, edgesecond_delta, edgegain_delta, edgeshift_delta, nodefirst_delta, nodebias_delta, nodesecond_delta, nodegain_delta, nodeshift_delta)
    return (local_delta, ghost_delta, edge_result, partials)

def reference(node_state, edge_state, senders, receivers, send_index, node_cotangent, edge_cotangent, edge_first, edge_bias, edge_second, edge_gain, edge_shift, node_first, node_bias, node_second, node_gain):
    features = node_state.shape[0]
    partition = jnp.arange(PARTITIONS, dtype=jnp.int32)[:, None]
    peer_slot = jnp.arange(PEERS, dtype=jnp.int32)[None, :]
    slot_position = jnp.arange(HALO, dtype=jnp.int32)[None, None, :]
    mirror_slot = peer_slot // N_SUB * N_SUB + partition % N_SUB
    source_row = partition // N_SUB + 1 - peer_slot // N_SUB
    source_ok = (source_row >= 0) & (source_row < N_DOM)
    source = jnp.clip(source_row * N_SUB + peer_slot % N_SUB, 0, PARTITIONS - 1)
    incoming = send_index[source, mirror_slot]
    live_in = source_ok[:, :, None] & (incoming >= 0)
    global_in = source[:, :, None] * CELLS_DEV + jnp.maximum(incoming, 0)
    gathered = jnp.take(node_state, global_in.reshape(-1).astype(jnp.int32), axis=1)
    ghost_cells = jnp.where(live_in.reshape(1, -1), gathered, jnp.zeros_like(gathered))
    weight_shapes = (edge_first.shape, edge_bias.shape, edge_second.shape, edge_gain.shape, edge_gain.shape, node_first.shape, node_bias.shape, node_second.shape, node_gain.shape, node_gain.shape)
    initial = (jnp.zeros((features, CELLS), jnp.float32), jnp.zeros((features, PARTITIONS * GHOST), jnp.float32), jnp.zeros((features, FACES), jnp.bfloat16), tuple((jnp.zeros(shape, jnp.float32) for shape in weight_shapes)))

    def one_partition(loop_index, carried):
        local_all, ghost_all, edge_all, weight_all = carried
        cell_start = (loop_index * CELLS_DEV).astype(jnp.int32)
        face_start = (loop_index * FACES_DEV).astype(jnp.int32)
        ghost_start = (loop_index * GHOST).astype(jnp.int32)
        state_block = lax.dynamic_slice_in_dim(node_state, cell_start, CELLS_DEV, 1)
        ghost_block = lax.dynamic_slice_in_dim(ghost_cells, ghost_start, GHOST, 1)
        extended = jnp.concatenate([state_block, ghost_block], axis=1)
        outcome = local_backward(extended, state_block, lax.dynamic_slice_in_dim(edge_state, face_start, FACES_DEV, 1), lax.dynamic_slice_in_dim(senders, face_start, FACES_DEV, 0), lax.dynamic_slice_in_dim(receivers, face_start, FACES_DEV, 0), lax.dynamic_slice_in_dim(node_cotangent, cell_start, CELLS_DEV, 1), lax.dynamic_slice_in_dim(edge_cotangent, face_start, FACES_DEV, 1), edge_first, edge_bias, edge_second, edge_gain, edge_shift, node_first, node_bias, node_second, node_gain)
        local_delta, ghost_delta, edge_result, partials = outcome
        local_all = lax.dynamic_update_slice_in_dim(local_all, local_delta, cell_start, 1)
        ghost_all = lax.dynamic_update_slice_in_dim(ghost_all, ghost_delta, ghost_start, 1)
        edge_all = lax.dynamic_update_slice_in_dim(edge_all, edge_result, face_start, 1)
        weight_all = tuple((running + portion for running, portion in zip(weight_all, partials)))
        return (local_all, ghost_all, edge_all, weight_all)
    local_all, ghost_all, edge_all, weight_all = lax.fori_loop(0, PARTITIONS, one_partition, initial)
    target_row = partition // N_SUB + peer_slot // N_SUB - 1
    target_ok = (target_row >= 0) & (target_row < N_DOM)
    target = jnp.clip(target_row * N_SUB + peer_slot % N_SUB, 0, PARTITIONS - 1)
    live_out = target_ok[:, :, None] & (send_index >= 0)
    from_index = (target * PEERS + mirror_slot)[:, :, None] * HALO + slot_position
    coming_back = jnp.take(ghost_all, from_index.reshape(-1).astype(jnp.int32), axis=1)
    coming_back = jnp.where(live_out.reshape(1, -1), coming_back, jnp.zeros_like(coming_back))
    to_index = partition[:, :, None] * CELLS_DEV + jnp.maximum(send_index, 0)
    local_all = local_all.at[:, to_index.reshape(-1).astype(jnp.int32)].add(coming_back)
    factor = 1.0 / math.sqrt(FACES)
    edgefirst_sum, edgebias_sum, edgesecond_sum, edgegain_sum, edgeshift_sum, nodefirst_sum, nodebias_sum, nodesecond_sum, nodegain_sum, nodeshift_sum = weight_all
    return (local_all.astype(jnp.bfloat16), edge_all, edgefirst_sum * factor, edgebias_sum * factor, edgesecond_sum * factor, edgegain_sum * factor, edgeshift_sum * factor, nodefirst_sum * factor, nodebias_sum * factor, nodesecond_sum * factor, nodegain_sum * factor, nodeshift_sum * factor)
```

```python
import functools
import math

import jax
import jax.numpy as jnp
from jax import lax
from jax.experimental import pallas as pl
from jax.experimental.pallas import tpu as pltpu
from jax.sharding import PartitionSpec as P

EPSILON = 1e-05
LOW = 256
F32 = jnp.float32
BF16 = jnp.bfloat16
VECTORS = 6


def mm(a, b):
    return lax.dot_general(a, b, (((1,), (0,)), ((), ())), preferred_element_type=F32)


def mm_nt(a, b):
    return lax.dot_general(a, b, (((1,), (1,)), ((), ())), preferred_element_type=F32)


def low_hot(index):
    rows = lax.broadcasted_iota(jnp.int32, (LOW, index.shape[1]), 0)
    return jnp.where(rows == (index & (LOW - 1)), 1.0, 0.0).astype(BF16)


def pick_high(stack, index, features):
    high = index >> 8
    blocks = stack.shape[0] // features
    result = jnp.zeros((features, stack.shape[1]), stack.dtype)
    for number in range(blocks):
        part = stack[number * features : (number + 1) * features]
        result = jnp.where(high == number, part, result)
    return result


def spread_high(values, index, blocks):
    high = index >> 8
    zero = jnp.zeros_like(values)
    return jnp.concatenate(
        [jnp.where(high == number, values, zero).astype(BF16) for number in range(blocks)], axis=0
    )


def stack_table(table):
    return jnp.concatenate(
        [table[:, begin : begin + LOW] for begin in range(0, table.shape[1], LOW)], axis=0
    )


def unstack(stack, features):
    return jnp.concatenate(
        [stack[begin : begin + features] for begin in range(0, stack.shape[0], features)], axis=1
    )


def sigmoid(values):
    return 1.0 / (1.0 + jnp.exp(-values))


def standardize(values):
    centered = values - jnp.mean(values, axis=0, keepdims=True)
    spread = lax.rsqrt(jnp.mean(centered * centered, axis=0, keepdims=True) + EPSILON)
    return centered * spread, spread


def norm_back(upstream, scaled, spread, gain):
    weighted = upstream * gain
    return spread * (
        weighted
        - jnp.mean(weighted, axis=0, keepdims=True)
        - scaled * jnp.mean(weighted * scaled, axis=0, keepdims=True)
    )


def pair_rows(index_ref, first):
    return jnp.concatenate([index_ref[first : first + 1], index_ref[first + 1 : first + 2]], axis=1)


def pick_kernel(node_ref, index_ref, out_ref):
    features = node_ref.shape[0]
    subs = out_ref.shape[0]
    halo = index_ref.shape[1]
    table = stack_table(node_ref[...])
    for first in range(0, index_ref.shape[0], 2):
        index = pair_rows(index_ref, first)
        chosen = pick_high(mm(table, low_hot(index)), index, features).astype(BF16)
        for extra in range(2):
            block = first + extra
            out_ref[block % subs, block // subs] = chosen[:, extra * halo : (extra + 1) * halo]


def main_kernel(
    node_ref,
    across_ref,
    upper_ref,
    lower_ref,
    edge_ref,
    senders_ref,
    receivers_ref,
    nodecot_ref,
    edgecot_ref,
    edgefirst_ref,
    edgesecond_ref,
    nodefirst_ref,
    nodesecond_ref,
    vectors_ref,
    local_ref,
    ghost_ref,
    result_ref,
    partial_ref,
    table_ref,
    shot_ref,
    rhot_ref,
    slope_ref,
    active_ref,
    scaled_ref,
    spread_ref,
    *,
    tile,
    factor,
):
    features, cells = node_ref.shape
    faces = edge_ref.shape[1]
    subs, halo = upper_ref.shape[0], upper_ref.shape[2]
    own = cells // LOW
    total = table_ref.shape[0] // features
    vectors = vectors_ref[...]
    edge_bias, edge_gain, edge_shift, node_bias, node_gain = [
        vectors[:, number : number + 1] for number in range(5)
    ]
    first_t = edgefirst_ref[...]
    second = edgesecond_ref[...]
    second_t = second.astype(F32).T.astype(BF16)
    first = first_t.astype(F32).T.astype(BF16)

    node_state = node_ref[...]
    table_ref[: own * features] = stack_table(node_state)
    for block in range(3 * subs):
        source = (
            upper_ref[block % subs]
            if block < subs
            else (across_ref[block % subs, 1] if block < 2 * subs else lower_ref[block % subs])
        )
        column = block * halo
        row = (own + column // LOW) * features
        table_ref[row : row + features, column % LOW : column % LOW + halo] = source

    summed = jnp.zeros((own * features, LOW), F32)
    for begin in range(0, faces, tile):
        at = slice(begin, begin + tile)
        sender, receiver = senders_ref[:, at], receivers_ref[:, at]
        shot, rhot = low_hot(sender), low_hot(receiver)
        shot_ref[:, at] = shot
        rhot_ref[:, at] = rhot
        sender_rows = pick_high(mm(table_ref[...], shot), sender, features).astype(BF16)
        receiver_rows = pick_high(
            mm(table_ref[: own * features], rhot), receiver, features
        ).astype(BF16)
        stacked = jnp.concatenate([sender_rows, receiver_rows, edge_ref[:, at]], axis=0)
        linear = mm(first_t, stacked) + edge_bias
        logistic = sigmoid(linear)
        slope_ref[:, at] = logistic * (1.0 + linear * (1.0 - logistic))
        active = (linear * logistic).astype(BF16)
        active_ref[:, at] = active
        scaled, spread = standardize(mm(second_t, active))
        scaled_ref[:, at] = scaled
        spread_ref[:, at] = spread
        message = (scaled * edge_gain + edge_shift).astype(BF16).astype(F32)
        summed = summed + mm_nt(spread_high(message, receiver, own), rhot)

    node_first_t = nodefirst_ref[...]
    node_first = node_first_t.astype(F32).T.astype(BF16)
    node_second = nodesecond_ref[...]
    node_second_t = node_second.astype(F32).T.astype(BF16)
    node_input = jnp.concatenate([node_state, unstack(summed, features).astype(BF16)], axis=0)
    node_linear = mm(node_first_t, node_input) + node_bias
    node_logistic = sigmoid(node_linear)
    node_active = (node_linear * node_logistic).astype(BF16)
    node_scaled, node_spread = standardize(mm(node_second_t, node_active))
    upstream = nodecot_ref[...].astype(F32)
    nodegain_delta = jnp.sum(upstream * node_scaled, axis=1, keepdims=True)
    nodeshift_delta = jnp.sum(upstream, axis=1, keepdims=True)
    node_delta = norm_back(upstream, node_scaled, node_spread, node_gain).astype(BF16)
    nodesecond_delta = mm_nt(node_active, node_delta)
    node_hidden = mm(node_second, node_delta) * (
        node_logistic * (1.0 + node_linear * (1.0 - node_logistic))
    )
    nodebias_delta = jnp.sum(node_hidden, axis=1, keepdims=True)
    node_hidden = node_hidden.astype(BF16)
    nodefirst_delta = mm_nt(node_input, node_hidden)
    node_back = mm(node_first, node_hidden)
    local = upstream + node_back[:features]
    back_table = stack_table(node_back[features:]).astype(BF16)

    sender_sum = jnp.zeros((total * features, LOW), F32)
    receiver_sum = jnp.zeros((own * features, LOW), F32)
    gain_sum = jnp.zeros((features, tile), F32)
    shift_sum = jnp.zeros((features, tile), F32)
    bias_sum = jnp.zeros((features, tile), F32)
    edgesecond_delta = jnp.zeros((features, features), F32)
    edgethird_delta = jnp.zeros((features, features), F32)
    first_s, first_r, first_e = [
        first[number * features : (number + 1) * features] for number in range(3)
    ]
    for begin in range(0, faces, tile):
        at = slice(begin, begin + tile)
        sender, receiver = senders_ref[:, at], receivers_ref[:, at]
        shot, rhot = shot_ref[:, at], rhot_ref[:, at]
        cotangent = edgecot_ref[:, at].astype(F32)
        scaled = scaled_ref[:, at]
        message_delta = cotangent + pick_high(mm(back_table, rhot), receiver, features)
        gain_sum = gain_sum + message_delta * scaled
        shift_sum = shift_sum + message_delta
        delta = norm_back(message_delta, scaled, spread_ref[:, at], edge_gain).astype(BF16)
        edgesecond_delta = edgesecond_delta + mm_nt(active_ref[:, at], delta)
        hidden = mm(second, delta) * slope_ref[:, at]
        bias_sum = bias_sum + hidden
        rounded = hidden.astype(BF16)
        result_ref[:, at] = (cotangent + mm(first_e, rounded)).astype(BF16)
        edgethird_delta = edgethird_delta + mm_nt(edge_ref[:, at], rounded)
        wide = rounded.astype(F32)
        sender_sum = sender_sum + mm_nt(spread_high(wide, sender, total), shot)
        receiver_sum = receiver_sum + mm_nt(spread_high(wide, receiver, own), rhot)

    sender_sum = sender_sum.astype(BF16)
    receiver_sum = unstack(receiver_sum, features).astype(BF16)
    edgefirst_s = jnp.zeros((features, features), F32)
    for number in range(total):
        rows = slice(number * features, (number + 1) * features)
        edgefirst_s = edgefirst_s + mm_nt(table_ref[rows], sender_sum[rows])
    edgefirst_r = mm_nt(node_state, receiver_sum)
    spread_out = mm(first_s, unstack(sender_sum, features))
    local_ref[...] = local + spread_out[:, :cells] + mm(first_r, receiver_sum)
    for block in range(3 * subs):
        column = cells + block * halo
        ghost_ref[block % subs, block // subs] = spread_out[:, column : column + halo].astype(BF16)

    columns = [
        jnp.sum(bias_sum, axis=1, keepdims=True),
        jnp.sum(gain_sum, axis=1, keepdims=True),
        jnp.sum(shift_sum, axis=1, keepdims=True),
        nodebias_delta,
        nodegain_delta,
        nodeshift_delta,
    ]
    lanes = lax.broadcasted_iota(jnp.int32, (features, features), 1)
    vector_block = jnp.zeros((features, features), F32)
    for number, column in enumerate(columns):
        vector_block = jnp.where(lanes == number, column, vector_block)
    pairs = (
        (edgefirst_s, edgefirst_r),
        (edgethird_delta, edgesecond_delta),
        (nodefirst_delta[:features], nodefirst_delta[features:]),
        (nodesecond_delta, vector_block),
    )
    for number, (left, right) in enumerate(pairs):
        partial_ref[number * features : (number + 1) * features] = (
            jnp.concatenate([left, right], axis=1) * factor
        )


def final_kernel(
    local_ref,
    across_ref,
    further_ref,
    nearer_ref,
    index_ref,
    totals_ref,
    state_ref,
    edgefirst_ref,
    edgesecond_ref,
    nodefirst_ref,
    nodesecond_ref,
    vector_ref,
):
    features, cells = local_ref.shape
    subs = further_ref.shape[0]
    own = cells // LOW

    def returned(block):
        group = block // subs
        if group == 0:
            return further_ref[block % subs]
        if group == 1:
            return across_ref[block % subs, 1]
        return nearer_ref[block % subs]

    total = jnp.zeros((own * features, LOW), F32)
    for first in range(0, index_ref.shape[0], 2):
        index = pair_rows(index_ref, first)
        values = jnp.concatenate([returned(first), returned(first + 1)], axis=1).astype(F32)
        total = total + mm_nt(spread_high(values, index, own), low_hot(index))
    state_ref[...] = (local_ref[...] + unstack(total, features)).astype(BF16)

    sums = [totals_ref[number * features : (number + 1) * features] for number in range(4)]
    halves = [(part[:, :features], part[:, features:]) for part in sums]
    edgefirst_ref[...] = jnp.concatenate([halves[0][0], halves[0][1], halves[1][0]], axis=0).T
    edgesecond_ref[...] = halves[1][1]
    nodefirst_ref[...] = jnp.concatenate([halves[2][0], halves[2][1]], axis=0).T
    nodesecond_ref[...] = halves[3][0]
    vector_ref[...] = halves[3][1].T[: vector_ref.shape[0]]


def shift(value, steps):
    count = lax.axis_size("dom")
    first, last = max(0, -steps), min(count, count - steps)
    return lax.ppermute(value, "dom", [(source, source + steps) for source in range(first, last)])


def exchange(blocks):
    across = lax.all_to_all(blocks, "sub", split_axis=0, concat_axis=0, tiled=True)
    return across, across[:, 0], across[:, 2]


def total_over(value):
    for axis in ("sub", "dom"):
        count = lax.axis_size(axis)
        if count & (count - 1):
            value = lax.psum(value, axis)
            continue
        step = 1
        while step < count:
            value = value + lax.ppermute(value, axis, [(i, i ^ step) for i in range(count)])
            step *= 2
    return value


def on_device(
    node_state,
    edge_state,
    senders,
    receivers,
    send_index,
    node_cotangent,
    edge_cotangent,
    edge_first,
    edge_bias,
    edge_second,
    edge_gain,
    edge_shift,
    node_first,
    node_bias,
    node_second,
    node_gain,
):
    features, cells = node_state.shape
    faces = edge_state.shape[1]
    subs = lax.axis_size("sub")
    halo = send_index.shape[2]
    blocks = 3 * subs
    index = send_index.reshape(blocks, halo)
    faces_total = faces * lax.axis_size("dom") * subs
    factor = 1.0 / math.sqrt(faces_total)
    wide = cells + blocks * halo
    tile = math.gcd(faces, 512)
    shape = jax.ShapeDtypeStruct
    ghost_shape = shape((subs, 3, features, halo), BF16)

    outgoing = pl.pallas_call(pick_kernel, out_shape=ghost_shape, name="pick")(node_state, index)
    across, up, down = exchange(outgoing)
    upper, lower = shift(up, -1), shift(down, 1)
    vectors = jnp.stack([edge_bias, edge_gain, edge_shift, node_bias, node_gain], axis=1)
    local, ghost, edge_result, partial = pl.pallas_call(
        functools.partial(main_kernel, tile=tile, factor=factor),
        out_shape=(
            shape((features, cells), F32),
            ghost_shape,
            shape((features, faces), BF16),
            shape((4 * features, 2 * features), F32),
        ),
        scratch_shapes=[
            pltpu.VMEM((wide // LOW * features, LOW), BF16),
            pltpu.VMEM((LOW, faces), BF16),
            pltpu.VMEM((LOW, faces), BF16),
            pltpu.VMEM((features, faces), F32),
            pltpu.VMEM((features, faces), BF16),
            pltpu.VMEM((features, faces), F32),
            pltpu.VMEM((1, faces), F32),
        ],
        compiler_params=pltpu.CompilerParams(vmem_limit_bytes=48 * 1024 * 1024),
        name="main",
    )(
        node_state,
        across,
        upper,
        lower,
        edge_state,
        senders.reshape(1, faces),
        receivers.reshape(1, faces),
        node_cotangent,
        edge_cotangent,
        edge_first.T,
        edge_second,
        node_first.T,
        node_second,
        vectors,
    )
    returned, forth, back = exchange(ghost)
    further, nearer = shift(forth, 1), shift(back, -1)
    totals = total_over(partial)
    state, edgefirst, edgesecond, nodefirst, nodesecond, vector = pl.pallas_call(
        final_kernel,
        out_shape=(
            shape((features, cells), BF16),
            shape((features, 3 * features), F32),
            shape((features, features), F32),
            shape((features, 2 * features), F32),
            shape((features, features), F32),
            shape((VECTORS, features), F32),
        ),
        name="final",
    )(local, returned, further, nearer, index, totals)
    return (
        state,
        edge_result,
        edgefirst.T,
        vector[0],
        edgesecond,
        vector[1],
        vector[2],
        nodefirst.T,
        vector[3],
        nodesecond,
        vector[4],
        vector[5],
    )


def solution(mesh):
    parts = ("dom", "sub")
    columns = P(None, parts)
    in_specs = (columns, columns, P(parts), P(parts), P(parts, None, None), columns, columns)
    in_specs = in_specs + (P(),) * 9
    out_specs = (columns, columns) + (P(),) * 10
    return jax.shard_map(
        on_device, mesh=mesh, in_specs=in_specs, out_specs=out_specs, check_vma=False
    )
```

```python
import functools
import math

import jax
import jax.numpy as jnp
from jax import lax
from jax.experimental import pallas as pl
from jax.experimental.pallas import tpu as pltpu
from jax.sharding import PartitionSpec as P

EPSILON = 1e-05
LOW = 256
F32 = jnp.float32
BF16 = jnp.bfloat16
VECTORS = 6


def mm(a, b):
    return lax.dot_general(a, b, (((1,), (0,)), ((), ())), preferred_element_type=F32)


def mm_nt(a, b):
    return lax.dot_general(a, b, (((1,), (1,)), ((), ())), preferred_element_type=F32)


def low_hot(index):
    rows = lax.broadcasted_iota(jnp.int32, (LOW, index.shape[1]), 0)
    return jnp.where(rows == (index & (LOW - 1)), 1.0, 0.0).astype(BF16)


def pick_high(stack, index, features):
    high = index >> 8
    blocks = stack.shape[0] // features
    result = jnp.zeros((features, stack.shape[1]), stack.dtype)
    for number in range(blocks):
        part = stack[number * features : (number + 1) * features]
        result = jnp.where(high == number, part, result)
    return result


def spread_high(values, index, blocks):
    high = index >> 8
    zero = jnp.zeros_like(values)
    return jnp.concatenate(
        [jnp.where(high == number, values, zero).astype(BF16) for number in range(blocks)], axis=0
    )


def stack_table(table):
    return jnp.concatenate(
        [table[:, begin : begin + LOW] for begin in range(0, table.shape[1], LOW)], axis=0
    )


def unstack(stack, features):
    return jnp.concatenate(
        [stack[begin : begin + features] for begin in range(0, stack.shape[0], features)], axis=1
    )


def sigmoid(values):
    return 1.0 / (1.0 + jnp.exp(-values))


def standardize(values):
    centered = values - jnp.mean(values, axis=0, keepdims=True)
    spread = lax.rsqrt(jnp.mean(centered * centered, axis=0, keepdims=True) + EPSILON)
    return centered * spread, spread


def norm_back(upstream, scaled, spread, gain):
    weighted = upstream * gain
    return spread * (
        weighted
        - jnp.mean(weighted, axis=0, keepdims=True)
        - scaled * jnp.mean(weighted * scaled, axis=0, keepdims=True)
    )


def pair_rows(index_ref, first):
    return jnp.concatenate([index_ref[first], index_ref[first + 1]], axis=1)


def pick_kernel(node_ref, index_ref, out_ref):
    features = node_ref.shape[0]
    subs = out_ref.shape[0]
    halo = index_ref.shape[2]
    table = stack_table(node_ref[...])
    for first in range(0, index_ref.shape[0], 2):
        index = pair_rows(index_ref, first)
        chosen = pick_high(mm(table, low_hot(index)), index, features).astype(BF16)
        for extra in range(2):
            block = first + extra
            out_ref[block % subs, block // subs] = chosen[:, extra * halo : (extra + 1) * halo]


def fill_table(table_ref, node_state, across_ref, upper_ref, lower_ref):
    features, cells = node_state.shape
    subs, halo = upper_ref.shape[0], upper_ref.shape[2]
    own = cells // LOW
    table_ref[: own * features] = stack_table(node_state)
    for block in range(3 * subs):
        source = (
            upper_ref[block % subs]
            if block < subs
            else (across_ref[block % subs, 1] if block < 2 * subs else lower_ref[block % subs])
        )
        column = block * halo
        row = (own + column // LOW) * features
        table_ref[row : row + features, column % LOW : column % LOW + halo] = source


def flip(matrix):
    return matrix.astype(F32).T.astype(BF16)


def early_kernel(
    node_ref, edge_ref, senders_ref, receivers_ref, edgefirst_ref, vectors_ref, linear_ref, *, tile
):
    features = node_ref.shape[0]
    table = stack_table(node_ref[...])
    first_t = edgefirst_ref[...]
    edge_bias = vectors_ref[:, 0:1]
    for begin in range(0, edge_ref.shape[1], tile):
        at = slice(begin, begin + tile)
        sender, receiver = senders_ref[:, at], receivers_ref[:, at]
        sender_rows = pick_high(mm(table, low_hot(sender)), sender, features).astype(BF16)
        receiver_rows = pick_high(mm(table, low_hot(receiver)), receiver, features).astype(BF16)
        stacked = jnp.concatenate([sender_rows, receiver_rows, edge_ref[:, at]], axis=0)
        linear_ref[:, at] = mm(first_t, stacked) + edge_bias


def main_kernel(
    linear_ref,
    node_ref,
    across_ref,
    upper_ref,
    lower_ref,
    senders_ref,
    receivers_ref,
    nodecot_ref,
    edgecot_ref,
    edgefirst_ref,
    edgesecond_ref,
    nodefirst_ref,
    nodesecond_ref,
    vectors_ref,
    ghost_ref,
    local_ref,
    sum_ref,
    active_ref,
    delta_ref,
    hidden_ref,
    partial_ref,
    table_ref,
    shot_ref,
    rhot_ref,
    slope_ref,
    scaled_ref,
    spread_ref,
    *,
    tile,
    factor,
):
    features, cells = node_ref.shape
    faces = senders_ref.shape[1]
    subs, halo = upper_ref.shape[0], upper_ref.shape[2]
    own = cells // LOW
    total = table_ref.shape[0] // features
    vectors = vectors_ref[...]
    edge_gain, edge_shift, node_bias, node_gain = [
        vectors[:, number : number + 1] for number in range(1, 5)
    ]
    first_st = edgefirst_ref[:, :features]
    second = edgesecond_ref[...]
    second_t = flip(second)
    first_s = flip(first_st)
    node_state = node_ref[...]
    fill_table(table_ref, node_state, across_ref, upper_ref, lower_ref)

    summed = jnp.zeros((own * features, LOW), F32)
    for begin in range(0, faces, tile):
        at = slice(begin, begin + tile)
        sender, receiver = senders_ref[:, at], receivers_ref[:, at]
        shot, rhot = low_hot(sender), low_hot(receiver)
        shot_ref[:, at] = shot
        rhot_ref[:, at] = rhot
        ghost_rows = pick_high(
            mm(table_ref[own * features :], shot), sender - cells, features
        ).astype(BF16)
        linear = linear_ref[:, at] + mm(first_st, ghost_rows)
        logistic = sigmoid(linear)
        slope_ref[:, at] = logistic * (1.0 + linear * (1.0 - logistic))
        active = (linear * logistic).astype(BF16)
        active_ref[:, at] = active
        scaled, spread = standardize(mm(second_t, active))
        scaled_ref[:, at] = scaled
        spread_ref[:, at] = spread
        message = (scaled * edge_gain + edge_shift).astype(BF16).astype(F32)
        summed = summed + mm_nt(spread_high(message, receiver, own), rhot)

    node_first_t = nodefirst_ref[...]
    node_first = flip(node_first_t)
    node_second = nodesecond_ref[...]
    node_second_t = flip(node_second)
    node_input = jnp.concatenate([node_state, unstack(summed, features).astype(BF16)], axis=0)
    node_linear = mm(node_first_t, node_input) + node_bias
    node_logistic = sigmoid(node_linear)
    node_active = (node_linear * node_logistic).astype(BF16)
    node_scaled, node_spread = standardize(mm(node_second_t, node_active))
    upstream = nodecot_ref[...].astype(F32)
    nodegain_delta = jnp.sum(upstream * node_scaled, axis=1, keepdims=True)
    nodeshift_delta = jnp.sum(upstream, axis=1, keepdims=True)
    node_delta = norm_back(upstream, node_scaled, node_spread, node_gain).astype(BF16)
    nodesecond_delta = mm_nt(node_active, node_delta)
    node_hidden = mm(node_second, node_delta) * (
        node_logistic * (1.0 + node_linear * (1.0 - node_logistic))
    )
    nodebias_delta = jnp.sum(node_hidden, axis=1, keepdims=True)
    node_hidden = node_hidden.astype(BF16)
    nodefirst_delta = mm_nt(node_input, node_hidden)
    node_back = mm(node_first, node_hidden)
    local = upstream + node_back[:features]
    back_table = stack_table(node_back[features:]).astype(BF16)

    sender_sum = jnp.zeros((total * features, LOW), F32)
    gain_sum = jnp.zeros((features, tile), F32)
    shift_sum = jnp.zeros((features, tile), F32)
    bias_sum = jnp.zeros((features, tile), F32)
    for begin in range(0, faces, tile):
        at = slice(begin, begin + tile)
        sender, receiver = senders_ref[:, at], receivers_ref[:, at]
        scaled = scaled_ref[:, at]
        message_delta = edgecot_ref[:, at].astype(F32) + pick_high(
            mm(back_table, rhot_ref[:, at]), receiver, features
        )
        gain_sum = gain_sum + message_delta * scaled
        shift_sum = shift_sum + message_delta
        delta = norm_back(message_delta, scaled, spread_ref[:, at], edge_gain).astype(BF16)
        delta_ref[:, at] = delta
        hidden = mm(second, delta) * slope_ref[:, at]
        bias_sum = bias_sum + hidden
        rounded = hidden.astype(BF16)
        hidden_ref[:, at] = rounded
        sender_sum = sender_sum + mm_nt(
            spread_high(rounded.astype(F32), sender, total), shot_ref[:, at]
        )

    sender_sum = sender_sum.astype(BF16)
    sum_ref[...] = sender_sum
    spread_out = mm(first_s, unstack(sender_sum, features))
    local_ref[...] = local + spread_out[:, :cells]
    for block in range(3 * subs):
        column = cells + block * halo
        ghost_ref[block % subs, block // subs] = spread_out[:, column : column + halo].astype(BF16)

    columns = [
        jnp.sum(bias_sum, axis=1, keepdims=True),
        jnp.sum(gain_sum, axis=1, keepdims=True),
        jnp.sum(shift_sum, axis=1, keepdims=True),
        nodebias_delta,
        nodegain_delta,
        nodeshift_delta,
    ]
    lanes = lax.broadcasted_iota(jnp.int32, (features, features), 1)
    vector_block = jnp.zeros((features, features), F32)
    for number, column in enumerate(columns):
        vector_block = jnp.where(lanes == number, column, vector_block)
    pairs = (
        (nodefirst_delta[:features], nodefirst_delta[features:]),
        (nodesecond_delta, vector_block),
    )
    for number, (left, right) in enumerate(pairs):
        partial_ref[number * features : (number + 1) * features] = (
            jnp.concatenate([left, right], axis=1) * factor
        )


def late_kernel(
    local_ref,
    sum_ref,
    active_ref,
    delta_ref,
    hidden_ref,
    node_partial_ref,
    node_ref,
    across_ref,
    upper_ref,
    lower_ref,
    edge_ref,
    receivers_ref,
    edgecot_ref,
    edgefirst_ref,
    partial_ref,
    result_ref,
    state_ref,
    table_ref,
    *,
    tile,
    factor,
):
    features, cells = node_ref.shape
    faces = edge_ref.shape[1]
    own = cells // LOW
    total = table_ref.shape[0] // features
    node_state = node_ref[...]
    fill_table(table_ref, node_state, across_ref, upper_ref, lower_ref)
    first = flip(edgefirst_ref[...])
    first_r, first_e = first[features : 2 * features], first[2 * features :]
    receiver_sum = jnp.zeros((own * features, LOW), F32)
    edgesecond_delta = jnp.zeros((features, features), F32)
    edgethird_delta = jnp.zeros((features, features), F32)
    for begin in range(0, faces, tile):
        at = slice(begin, begin + tile)
        receiver = receivers_ref[:, at]
        rounded = hidden_ref[:, at]
        edgesecond_delta = edgesecond_delta + mm_nt(active_ref[:, at], delta_ref[:, at])
        edgethird_delta = edgethird_delta + mm_nt(edge_ref[:, at], rounded)
        result_ref[:, at] = (edgecot_ref[:, at].astype(F32) + mm(first_e, rounded)).astype(BF16)
        receiver_sum = receiver_sum + mm_nt(
            spread_high(rounded.astype(F32), receiver, own), low_hot(receiver)
        )
    receiver_sum = unstack(receiver_sum, features).astype(BF16)
    edgefirst_s = jnp.zeros((features, features), F32)
    for number in range(total):
        rows = slice(number * features, (number + 1) * features)
        edgefirst_s = edgefirst_s + mm_nt(table_ref[rows], sum_ref[rows])
    edgefirst_r = mm_nt(node_state, receiver_sum)
    state_ref[...] = local_ref[...] + mm(first_r, receiver_sum)
    pairs = ((edgefirst_s, edgefirst_r), (edgethird_delta, edgesecond_delta))
    for number, (left, right) in enumerate(pairs):
        partial_ref[number * features : (number + 1) * features] = (
            jnp.concatenate([left, right], axis=1) * factor
        )
    partial_ref[2 * features :] = node_partial_ref[...]


def final_kernel(
    local_ref,
    across_ref,
    further_ref,
    nearer_ref,
    index_ref,
    totals_ref,
    state_ref,
    edgefirst_ref,
    edgesecond_ref,
    nodefirst_ref,
    nodesecond_ref,
    *vector_refs,
):
    features, cells = local_ref.shape
    subs = further_ref.shape[0]
    own = cells // LOW

    def returned(block):
        group = block // subs
        if group == 0:
            return further_ref[block % subs]
        if group == 1:
            return across_ref[block % subs, 1]
        return nearer_ref[block % subs]

    total = jnp.zeros((own * features, LOW), F32)
    for first in range(0, index_ref.shape[0], 2):
        index = pair_rows(index_ref, first)
        values = jnp.concatenate([returned(first), returned(first + 1)], axis=1).astype(F32)
        total = total + mm_nt(spread_high(values, index, own), low_hot(index))
    state_ref[...] = (local_ref[...] + unstack(total, features)).astype(BF16)

    sums = [totals_ref[number * features : (number + 1) * features] for number in range(4)]
    halves = [(part[:, :features], part[:, features:]) for part in sums]
    edgefirst_ref[...] = jnp.concatenate([halves[0][0], halves[0][1], halves[1][0]], axis=0).T
    edgesecond_ref[...] = halves[1][1]
    nodefirst_ref[...] = jnp.concatenate([halves[2][0], halves[2][1]], axis=0).T
    nodesecond_ref[...] = halves[3][0]
    rows = halves[3][1].T
    for number, vector_ref in enumerate(vector_refs):
        vector_ref[...] = rows[number : number + 1]


def shift(value, steps):
    count = lax.axis_size("dom")
    first, last = max(0, -steps), min(count, count - steps)
    return lax.ppermute(value, "dom", [(source, source + steps) for source in range(first, last)])


def exchange(blocks):
    across = lax.all_to_all(blocks, "sub", split_axis=0, concat_axis=0, tiled=True)
    return across, across[:, 0], across[:, 2]


def total_over(value):
    for axis in ("dom", "sub"):
        count = lax.axis_size(axis)
        if count & (count - 1):
            value = lax.psum(value, axis)
            continue
        step = 1
        while step < count:
            value = value + lax.ppermute(value, axis, [(i, i ^ step) for i in range(count)])
            step *= 2
    return value


def on_device(
    node_state,
    edge_state,
    senders,
    receivers,
    send_index,
    node_cotangent,
    edge_cotangent,
    edge_first,
    edge_bias,
    edge_second,
    edge_gain,
    edge_shift,
    node_first,
    node_bias,
    node_second,
    node_gain,
):
    features, cells = node_state.shape
    faces = edge_state.shape[1]
    subs = lax.axis_size("sub")
    halo = send_index.shape[2]
    blocks = 3 * subs
    index = send_index.reshape(blocks, 1, halo)
    faces_total = faces * lax.axis_size("dom") * subs
    factor = 1.0 / math.sqrt(faces_total)
    wide = cells + blocks * halo
    tile = math.gcd(faces, 512)
    shape = jax.ShapeDtypeStruct
    ghost_shape = shape((subs, 3, features, halo), BF16)

    outgoing = pl.pallas_call(pick_kernel, out_shape=ghost_shape, name="pick")(node_state, index)
    across, up, down = exchange(outgoing)
    upper, lower = shift(up, -1), shift(down, 1)
    vectors = jnp.stack([edge_bias, edge_gain, edge_shift, node_bias, node_gain], axis=1)
    senders, receivers = senders.reshape(1, faces), receivers.reshape(1, faces)
    edge_first, node_first = edge_first.T, node_first.T
    params = pltpu.CompilerParams(vmem_limit_bytes=48 * 1024 * 1024)
    linear = pl.pallas_call(
        functools.partial(early_kernel, tile=tile),
        out_shape=shape((features, faces), F32),
        compiler_params=params,
        cost_estimate=pl.CostEstimate(flops=1 << 31, transcendentals=0, bytes_accessed=1 << 21),
        name="early",
    )(node_state, edge_state, senders, receivers, edge_first, vectors)
    face_rows = shape((features, faces), BF16)
    ghost, local, sender_sum, active, delta, hidden, node_partial = pl.pallas_call(
        functools.partial(main_kernel, tile=tile, factor=factor),
        out_shape=(
            ghost_shape,
            shape((features, cells), F32),
            shape((wide // LOW * features, LOW), BF16),
            face_rows,
            face_rows,
            face_rows,
            shape((2 * features, 2 * features), F32),
        ),
        scratch_shapes=[
            pltpu.VMEM((wide // LOW * features, LOW), BF16),
            pltpu.VMEM((LOW, faces), BF16),
            pltpu.VMEM((LOW, faces), BF16),
            pltpu.VMEM((features, faces), F32),
            pltpu.VMEM((features, faces), F32),
            pltpu.VMEM((1, faces), F32),
        ],
        compiler_params=params,
        name="main",
    )(
        linear,
        node_state,
        across,
        upper,
        lower,
        senders,
        receivers,
        node_cotangent,
        edge_cotangent,
        edge_first,
        edge_second,
        node_first,
        node_second,
        vectors,
    )
    partial, edge_result, local = pl.pallas_call(
        functools.partial(late_kernel, tile=tile, factor=factor),
        out_shape=(
            shape((4 * features, 2 * features), F32),
            face_rows,
            shape((features, cells), F32),
        ),
        scratch_shapes=[pltpu.VMEM((wide // LOW * features, LOW), BF16)],
        compiler_params=params,
        cost_estimate=pl.CostEstimate(flops=1 << 31, transcendentals=0, bytes_accessed=1 << 21),
        name="late",
    )(
        local,
        sender_sum,
        active,
        delta,
        hidden,
        node_partial,
        node_state,
        across,
        upper,
        lower,
        edge_state,
        receivers,
        edge_cotangent,
        edge_first,
    )
    shifted = (shift(ghost[:, 0], 1), ghost[:, 1], shift(ghost[:, 2], -1))
    returned, further, nearer = exchange(jnp.stack(shifted, axis=1))
    totals = total_over(partial)
    state, edgefirst, edgesecond, nodefirst, nodesecond, *vector = pl.pallas_call(
        final_kernel,
        out_shape=(
            shape((features, cells), BF16),
            shape((features, 3 * features), F32),
            shape((features, features), F32),
            shape((features, 2 * features), F32),
            shape((features, features), F32),
        )
        + (shape((1, features), F32),) * VECTORS,
        name="final",
    )(local, returned, further, nearer, index, totals)
    vector = [row.reshape(features) for row in vector]
    return (
        state,
        edge_result,
        edgefirst.T,
        vector[0],
        edgesecond,
        vector[1],
        vector[2],
        nodefirst.T,
        vector[3],
        nodesecond,
        vector[4],
        vector[5],
    )


def solution(mesh):
    parts = ("dom", "sub")
    columns = P(None, parts)
    in_specs = (columns, columns, P(parts), P(parts), P(parts, None, None), columns, columns)
    in_specs = in_specs + (P(),) * 9
    out_specs = (columns, columns) + (P(),) * 10
    return jax.shard_map(
        on_device, mesh=mesh, in_specs=in_specs, out_specs=out_specs, check_vma=False
    )
```
